32 devices in a mesh: col: 4 (over y, x), tile: 8 (over z, core).
Axes of the slice: x: 2, y: 2, z: 4, core: 2. Of those that a mesh axis runs over, the one named last changes fastest.
Arguments:
- acquired: float32 [8192, 2, 1, 4096], P('tile', None, None, 'col'), may hold values from -6 to 6
- flatfield: float32 [2, 1024], replicated, may hold values from 0.5 to 1.5
- tile_gain: float32 [8, 4, 2], P('tile', 'col'), may hold values from 0.5 to 2
- subvoxel: float32 [8, 4, 2], P('tile', 'col'), may hold values from 0 to 1
- band_offset: int32 [8, 4, 2], P('tile', 'col'), may hold values from -2 to 2
- row_owner: int32 [8, 4, 1024, 1], P('tile', 'col'), may hold values from 0 to 31; in each aligned block of 1024 rows (0 to 1023, 1024 to 2047, ..., all dimensions but the last counted through in order) at most 48 rows name the same one
Outputs:
- owned_rows: float32 [49152, 2, 1, 1024], P(('col', 'tile'))
The draws below stay inside these ranges and needn't reach their ends.
Inputs may be any that keep to these rules, and one draw needn't show every extreme that they name: `row_owner`: no tile names one owner for more than 48 of its rows; some tile names some owner exactly 48 times.
All inputs are finite; a program needn't handle non-finite values.
Results may differ from the reference program's by a relative error of at most 0.0003.
Values sent between devices are 32-bit elements; how exact they have to be, the bound alone decides.
No kernel may reach another device: no remote copies, remote signals or barrier semaphores. Data moves between devices by JAX's collectives and lax.ppermute only.
A program may use at most 192 MiB of HBM per device.

```python
import math
import jax
import jax.numpy as jnp
import numpy as np
from jax import lax

TILE_H = 1024
TILE_W = 1024
CH = 2
MARGIN = 128
PLANES = 1
TILE_ROWS = 8
TILE_COLS = 4
TILES = 32
SLOTS = 48


def set_ends(values, key, least, top_value):
    longest = values.shape.index(max(values.shape))
    spots = []
    for shift in (0, 1):
        where = [jax.random.randint(jax.random.fold_in(key, axis), (), 0, length) for axis, length in enumerate(values.shape)]
        where[longest] = (where[longest] + shift) % values.shape[longest]
        spots.append(tuple(where))
    return values.at[spots[0]].set(least).at[spots[1]].set(top_value)


def shard_levels(stream_key, dims, pieces, least, largest):
    loudness, own = 1.0, jax.random.fold_in(stream_key, 6)
    for dim, parts in pieces:
        draws = jnp.exp(jax.random.uniform(jax.random.fold_in(own, dim), (parts,), jnp.float32, least / len(pieces), largest / len(pieces)))
        loudness = loudness * jnp.repeat(draws, dims[dim] // parts).reshape([-1 if axis == dim else 1 for axis in range(len(dims))])
    return loudness


def assign_block(stream_key, own, number, rows, count, top, limit, skew):
    sequence = jax.random.permutation(stream_key, count)
    heavy_load, ordinary = portions_of(count, rows * top, limit, skew, True), portions_of(count, rows * top, limit, skew, False)
    places = jnp.arange(count)

    def named(tallies, turn):
        used = int((tallies > 0).sum())
        fixed = max(1, used // 4)
        shifted = fixed + (places - fixed + turn * (used - fixed)) % max(1, count - fixed)
        return jnp.zeros((count,), jnp.int32).at[sequence[jnp.where(places < fixed, places, shifted)]].set(jnp.asarray(tallies, jnp.int32))

    tallies = jnp.where(number % 4 == 0, named(heavy_load, number // 4), named(ordinary, number - number // 4 - 1))
    mixed = jax.random.permutation(jax.random.fold_in(own, 3), count)
    source_of, receiver = mixed[0:count // 2 * 2:2], mixed[1:count // 2 * 2:2]
    margin = jnp.minimum(tallies[source_of] - 1, limit - tallies[receiver]) // 2
    margin = jnp.where((source_of == sequence[0]) | (receiver == sequence[0]) | (tallies[receiver] == 0), 0, jnp.maximum(margin, 0))
    shifted = jax.random.randint(jax.random.fold_in(own, 4), (count // 2,), 0, 1 << 20) % (margin + 1)
    tallies = tallies.at[source_of].add(-shifted).at[receiver].add(shifted)
    items = jnp.searchsorted(jnp.cumsum(tallies), jnp.arange(rows * top), side="right").astype(jnp.int32)
    listing = items.reshape(top, rows).T
    listing = listing[jax.random.permutation(jax.random.fold_in(own, 1), rows)]
    turn = jax.random.randint(jax.random.fold_in(own, 2), (rows, 1), 0, top)
    return jnp.take_along_axis(listing, (jnp.arange(top)[None, :] + turn) % top, axis=1)


def portions_of(number_of, total, most, lean, full):
    loads = [(1 << 20) // math.isqrt(grade ** lean) + 1 for grade in range(1, number_of + 1)]
    largest = most if full else min(most, max(-(-total // number_of), total * loads[0] // sum(loads)))
    least = 1 if total - largest >= number_of - 1 else 0
    given, surplus = [largest] + [least] * (number_of - 1), total - largest - least * (number_of - 1)
    while surplus > 0:
        candidates = [i for i in range(1, number_of) if given[i] < largest] or [i for i in range(1, number_of) if given[i] < most]
        whole, remaining = sum([loads[i] for i in candidates]), surplus
        for i in candidates:
            extra = min(most - given[i], max(1, remaining * loads[i] // whole), surplus)
            given[i] = given[i] + extra
            surplus = surplus - extra
    return np.array(given)


def bell_draw(stream_key, extent, scale, reach, cuts=(), held_as=jnp.bfloat16):
    values = scale * jax.random.normal(stream_key, extent, jnp.float32)
    if cuts:
        values = values * shard_levels(stream_key, extent, cuts, -0.22, 0.18)
    return jnp.clip(values, -reach, reach).astype(held_as)


def setup_inputs(seed: int = 0) -> dict:
    splits = jax.random.split(jax.random.key(seed), 7)
    acquired = bell_draw(splits[0], (TILE_ROWS * TILE_H, CH, PLANES, TILE_COLS * TILE_W), 1.0, 6.0, ((0, 8), (3, 4)), jnp.float32)
    flatfield = jnp.clip(1.0 + 0.1 * jax.random.normal(splits[1], (CH, TILE_W), jnp.float32), 0.5, 1.5)
    tile_gain = jnp.clip(jnp.exp(math.log(2.0) - 1.3862944 * jax.random.uniform(splits[2], (TILE_ROWS, TILE_COLS, CH), jnp.float32) ** shard_levels(splits[2], (TILE_ROWS, TILE_COLS, CH), ((0, 8), (1, 4)), -0.2, 0.2)), 0.5, 2.0)
    subvoxel = jnp.clip(1.0 * jax.random.uniform(splits[3], (TILE_ROWS, TILE_COLS, 2), jnp.float32) ** shard_levels(splits[3], (TILE_ROWS, TILE_COLS, 2), ((0, 8), (1, 4)), -0.2, 0.2), 0.0, 1.0)
    band_offset = set_ends(jax.random.randint(splits[4], (TILE_ROWS, TILE_COLS, 2), -2, 3), jax.random.fold_in(splits[4], 1), -2, 2).astype(jnp.int32)
    row_owner_keys = jax.random.split(jax.random.fold_in(splits[5], 1), TILE_ROWS * TILE_COLS * TILE_H // TILE_H)
    row_owner_turns = jax.random.permutation(jax.random.fold_in(splits[5], 3), TILE_ROWS * TILE_COLS * TILE_H // TILE_H)
    row_owner = jax.vmap(lambda own, number: assign_block(jax.random.fold_in(splits[5], 2), own, number, TILE_H, TILES, 1, SLOTS, 2))(row_owner_keys, row_owner_turns).reshape((TILE_ROWS, TILE_COLS, TILE_H, 1))
    return dict(acquired=acquired, flatfield=flatfield, tile_gain=tile_gain, subvoxel=subvoxel, band_offset=band_offset, row_owner=row_owner)


def cubic_matrix(fraction, offset, length):
    cube = fraction * fraction * fraction
    square = fraction * fraction
    weights = (-0.5 * cube + square - 0.5 * fraction,
               1.5 * cube - 2.5 * square + 1.0,
               -1.5 * cube + 2.0 * square + 0.5 * fraction,
               0.5 * cube - 0.5 * square)
    target = jnp.arange(length, dtype=jnp.int32)[:, None]
    source = jnp.arange(length, dtype=jnp.int32)[None, :]
    matrix = jnp.zeros((length, length), jnp.float32)
    for place, weight in zip((-1, 0, 1, 2), weights):
        picked = jnp.clip(target + offset + place, 0, length - 1)
        matrix = matrix + jnp.where(source == picked, weight, jnp.float32(0.0))
    return matrix


def blend_ramps(length, has_prev, has_next):
    place = jnp.arange(length).astype(jnp.float32)
    rising = jnp.square(jnp.sin(0.5 * math.pi * (place + 0.5) / MARGIN))
    falling = jnp.square(jnp.cos(0.5 * math.pi * (place - (length - MARGIN) + 0.5) / MARGIN))
    head = place < MARGIN
    tail = place >= length - MARGIN
    before = jnp.where(head, has_prev * (1.0 - rising), 0.0)
    own = jnp.where(head, has_prev * rising + 1.0 - has_prev,
                    jnp.where(tail, has_next * falling + 1.0 - has_next, 1.0))
    after = jnp.where(tail, has_next * (1.0 - falling), 0.0)
    return jnp.stack([before, own, after])


def resample_tile(tile, flatfield, gain, fraction_pair, offset_pair):
    height, channels, planes, columns = tile.shape
    corrected = tile * flatfield[None, :, None, :] * gain[None, :, None, None]
    row_matrix = cubic_matrix(fraction_pair[0], offset_pair[0], height)
    col_matrix = cubic_matrix(fraction_pair[1], offset_pair[1], columns)
    along_rows = jnp.dot(row_matrix, corrected.reshape(height, channels * planes * columns),
                         precision=lax.Precision.HIGHEST, preferred_element_type=jnp.float32)
    both_ways = jnp.dot(along_rows.reshape(height * channels * planes, columns), col_matrix.T,
                        precision=lax.Precision.HIGHEST, preferred_element_type=jnp.float32)
    return both_ways.reshape(height, channels, planes, columns)


def route_rows(rows, owner, devices, slots):
    onehot = (owner[:, None] == jnp.arange(devices, dtype=jnp.int32)[None, :]).astype(jnp.int32)
    earlier = jnp.cumsum(onehot, axis=0) - onehot
    rank = jnp.sum(earlier * onehot, axis=1).astype(jnp.int32)
    slot = (owner * slots + rank).astype(jnp.int32)
    empty = jnp.zeros((devices * slots,) + rows.shape[1:], rows.dtype)
    return empty.at[slot].set(rows)


def reference(acquired, flatfield, tile_gain, subvoxel, band_offset, row_owner):
    grid = acquired.reshape(TILE_ROWS, TILE_H, CH, PLANES, TILE_COLS, TILE_W)
    tiles = jnp.transpose(grid, (4, 0, 1, 2, 3, 5)).reshape(TILES, TILE_H, CH, PLANES, TILE_W)
    gains = jnp.transpose(tile_gain, (1, 0, 2)).reshape(TILES, CH)
    fractions = jnp.transpose(subvoxel, (1, 0, 2)).reshape(TILES, 2)
    offsets = jnp.transpose(band_offset, (1, 0, 2)).reshape(TILES, 2)
    owners = jnp.transpose(row_owner, (1, 0, 2, 3)).reshape(TILES, TILE_H)

    def one_tile(bundle):
        return resample_tile(bundle[0], flatfield, bundle[1], bundle[2], bundle[3])

    resampled = lax.map(one_tile, (tiles, gains, fractions, offsets))
    frames = resampled.reshape(TILE_COLS, TILE_ROWS, TILE_H, CH, PLANES, TILE_W)
    zero_rows = jnp.zeros_like(frames[:, :1, :MARGIN])
    prev_rows = jnp.concatenate([zero_rows, frames[:, :-1, TILE_H - MARGIN:]], axis=1)
    next_rows = jnp.concatenate([frames[:, 1:, :MARGIN], zero_rows], axis=1)
    tall = jnp.concatenate([prev_rows, frames, next_rows], axis=2)
    zero_cols = jnp.zeros_like(tall[:1, :, :, :, :, :MARGIN])
    prev_cols = jnp.concatenate([zero_cols, tall[:-1, :, :, :, :, TILE_W - MARGIN:]], axis=0)
    next_cols = jnp.concatenate([tall[1:, :, :, :, :, :MARGIN], zero_cols], axis=0)
    extended = jnp.concatenate([prev_cols, tall, next_cols], axis=5)

    row_place = jnp.arange(TILE_ROWS)
    col_place = jnp.arange(TILE_COLS)
    row_weights = jax.vmap(lambda first, last: blend_ramps(TILE_H, first, last))(
        (row_place > 0).astype(jnp.float32), (row_place < TILE_ROWS - 1).astype(jnp.float32))
    col_weights = jax.vmap(lambda first, last: blend_ramps(TILE_W, first, last))(
        (col_place > 0).astype(jnp.float32), (col_place < TILE_COLS - 1).astype(jnp.float32))
    joined = jnp.zeros(frames.shape, jnp.float32)
    for above in range(3):
        for beside in range(3):
            window = extended[:, :, above * MARGIN:above * MARGIN + TILE_H, :, :,
                              beside * MARGIN:beside * MARGIN + TILE_W]
            joined = joined + (row_weights[None, :, above, :, None, None, None]
                             * col_weights[:, None, beside, None, None, None, :]) * window
    joined_flat = joined.reshape(TILES, TILE_H, CH, PLANES, TILE_W)

    def one_route(bundle):
        return route_rows(bundle[0], bundle[1], TILES, SLOTS)

    sends = lax.map(one_route, (joined_flat, owners))
    arranged = sends.reshape(TILES, TILES, SLOTS, CH, PLANES, TILE_W)
    arranged = jnp.transpose(arranged, (1, 0, 2, 3, 4, 5))
    return arranged.reshape(TILES * TILES * SLOTS, CH, PLANES, TILE_W)
```

```python
import math

import jax
import jax.numpy as jnp
from jax import lax
from jax.experimental import pallas as pl
from jax.experimental.pallas import tpu as pltpu
from jax.sharding import PartitionSpec as P

MARGIN = 128
LANES = 128
TAPS = (-1, 0, 1, 2)


def cubic_weights(f):
    square = f * f
    cube = square * f
    return (
        -0.5 * cube + square - 0.5 * f,
        1.5 * cube - 2.5 * square + 1.0,
        -1.5 * cube + 2.0 * square + 0.5 * f,
        0.5 * cube - 0.5 * square,
    )


def resample_rows(sub, off, gain, owner, x, field, out, head, tail, left, right, source, count, *,
                  height, step_rows, window, slots, devices, planes):
    step = pl.program_id(0)
    per = out.shape[0] // step_rows
    blocks = out.shape[1]
    start = jnp.clip(step * step_rows - 4, 0, height - window)
    row_w = cubic_weights(sub[0])
    col_w = cubic_weights(sub[1])
    row_off = off[0]
    col_off = off[1]
    edge_steps = MARGIN // step_rows
    steps = height // step_rows

    @pl.when(step == 0)
    def _():
        @pl.loop(0, devices * slots)
        def _(s):
            source[s] = height

        @pl.loop(0, devices)
        def _(d):
            count[d] = 0

    lane = lax.broadcasted_iota(jnp.int32, (per, blocks, LANES), 2)
    block = lax.broadcasted_iota(jnp.int32, (per, blocks, LANES), 1)
    first_block = block == 0
    last_block = block == blocks - 1
    takes_up = [lane < col_off + k for k in TAPS]
    takes_down = [lane >= LANES + col_off + k for k in TAPS]
    turns = [(LANES - col_off - k) & (LANES - 1) for k in TAPS]
    scale = jnp.stack([field[c // planes] * gain[c // planes] for c in range(per)])

    @pl.loop(0, step_rows, unroll=8)
    def _(r):
        row = step * step_rows + r
        y = None
        for k, w in zip(TAPS, row_w):
            at = jnp.clip(row + row_off + k, 0, height - 1) - start
            part = x[pl.ds(at * per, per)] * w
            y = part if y is None else y + part
        y = y * scale
        up = jnp.where(last_block, y[:, blocks - 1 :, LANES - 1 :], pltpu.roll(y, blocks - 1, 1))
        down = jnp.where(first_block, y[:, :1, :1], pltpu.roll(y, 1, 1))
        z = None
        for k in range(4):
            mixed = jnp.where(takes_up[k], up, jnp.where(takes_down[k], down, y))
            part = pltpu.roll(mixed, turns[k], 2) * col_w[k]
            z = part if z is None else z + part
        out[pl.ds(r * per, per)] = z
        left[pl.ds(r * per, per), :] = z[:, 0, :]
        right[pl.ds(r * per, per), :] = z[:, blocks - 1, :]
        d = owner[row]
        rank = count[d]
        count[d] = rank + 1
        source[d * slots + rank] = row

    @pl.when(step < edge_steps)
    def _():
        head[...] = out[...]

    @pl.when(step >= steps - edge_steps)
    def _():
        tail[...] = out[...]


def blend_and_place(source, row_w, col_w, own, left, right, above, below, corner_al, corner_ar,
                    corner_bl, corner_br, out, joined, *, height, per):
    step = pl.program_id(0)

    @pl.when(step == 0)
    def _():
        before = col_w[0]
        mine = col_w[1]
        after = col_w[2]

        def across(mid, lo, hi, i):
            lo_v = jnp.broadcast_to(lo[pl.ds(i, 1), :], mine.shape)
            hi_v = jnp.broadcast_to(hi[pl.ds(i, 1), :], mine.shape)
            return mine * mid[i] + before * lo_v + after * hi_v

        @pl.loop(0, MARGIN * per, unroll=8)
        def _(i):
            r = i // per
            joined[i] = row_w[1, r] * across(own, left, right, i) + row_w[0, r] * across(
                above, corner_al, corner_ar, i)

        @pl.loop(MARGIN * per, (height - MARGIN) * per, unroll=8)
        def _(i):
            joined[i] = across(own, left, right, i)

        @pl.loop(0, MARGIN * per, unroll=8)
        def _(t):
            i = t + (height - MARGIN) * per
            r = i // per
            joined[i] = row_w[1, r] * across(own, left, right, i) + row_w[2, r] * across(
                below, corner_bl, corner_br, t)

        joined[height * per : (height + 1) * per] = jnp.zeros((per,) + joined.shape[1:], jnp.float32)

    here = out.shape[0] // per

    @pl.loop(0, here, unroll=8)
    def _(s):
        r = source[step * here + s]
        out[pl.ds(s * per, per)] = joined[pl.ds(r * per, per)]


def blend_ramps(length, has_prev, has_next):
    place = jnp.arange(length).astype(jnp.float32)
    rising = jnp.square(jnp.sin(0.5 * math.pi * (place + 0.5) / MARGIN))
    falling = jnp.square(jnp.cos(0.5 * math.pi * (place - (length - MARGIN) + 0.5) / MARGIN))
    head = place < MARGIN
    tail = place >= length - MARGIN
    before = jnp.where(head, has_prev * (1.0 - rising), 0.0)
    own = jnp.where(
        head,
        has_prev * rising + 1.0 - has_prev,
        jnp.where(tail, has_next * falling + 1.0 - has_next, 1.0),
    )
    after = jnp.where(tail, has_next * (1.0 - falling), 0.0)
    return jnp.stack([before, own, after])


def shards(acquired, flatfield, tile_gain, subvoxel, band_offset, row_owner):
    height, channels, planes, columns = acquired.shape
    per = channels * planes
    blocks = columns // LANES
    cols, tiles = lax.axis_size("col"), lax.axis_size("tile")
    devices = cols * tiles
    slots = max(2, (3 * height + 2 * devices - 1) // (2 * devices))
    f32 = jnp.float32
    smem = pl.BlockSpec(memory_space=pltpu.SMEM)

    step_rows = math.gcd(64, height)
    steps = height // step_rows
    window = step_rows + 8
    edge_steps = MARGIN // step_rows
    edge = MARGIN * per
    row_block = (step_rows * per, blocks, LANES)

    def window_start(i):
        return (jnp.clip(i * step_rows - 4, 0, height - window) * per, 0, 0)

    resampled, head, tail, left, right, source = pl.pallas_call(
        lambda *refs: resample_rows(*refs, height=height, step_rows=step_rows, window=window,
                                    slots=slots, devices=devices, planes=planes),
        grid=(steps,),
        in_specs=[
            smem, smem, smem, smem,
            pl.BlockSpec((pl.Element(window * per), pl.Element(blocks), pl.Element(LANES)), window_start),
            pl.BlockSpec((channels, blocks, LANES), lambda i: (0, 0, 0)),
        ],
        out_specs=[
            pl.BlockSpec(row_block, lambda i: (i, 0, 0)),
            pl.BlockSpec(row_block, lambda i: (jnp.minimum(i, edge_steps - 1), 0, 0)),
            pl.BlockSpec(row_block, lambda i: (jnp.maximum(i - (steps - edge_steps), 0), 0, 0)),
            pl.BlockSpec((step_rows * per, LANES), lambda i: (i, 0)),
            pl.BlockSpec((step_rows * per, LANES), lambda i: (i, 0)),
            smem,
        ],
        out_shape=[
            jax.ShapeDtypeStruct((height * per, blocks, LANES), f32),
            jax.ShapeDtypeStruct((edge, blocks, LANES), f32),
            jax.ShapeDtypeStruct((edge, blocks, LANES), f32),
            jax.ShapeDtypeStruct((height * per, LANES), f32),
            jax.ShapeDtypeStruct((height * per, LANES), f32),
            jax.ShapeDtypeStruct((devices * slots,), jnp.int32),
        ],
        scratch_shapes=[pltpu.SMEM((devices,), jnp.int32)],
        name="resample_rows",
    )(
        subvoxel.reshape(2),
        band_offset.reshape(2),
        tile_gain.reshape(channels),
        row_owner.reshape(height),
        acquired.reshape(height * per, blocks, LANES),
        flatfield.reshape(channels, blocks, LANES),
    )

    def shifted(value, dc, dt):
        pairs = []
        for c in range(cols):
            for t in range(tiles):
                if 0 <= c + dc < cols and 0 <= t + dt < tiles:
                    pairs.append((c * tiles + t, (c + dc) * tiles + t + dt))
        return lax.ppermute(value, ("col", "tile"), pairs)

    from_left = shifted(right, 1, 0)
    from_right = shifted(left, -1, 0)
    from_above = shifted(tail, 0, 1)
    from_below = shifted(head, 0, -1)
    corner_al = shifted(right[-edge:], 1, 1)
    corner_ar = shifted(left[-edge:], -1, 1)
    corner_bl = shifted(right[:edge], 1, -1)
    corner_br = shifted(left[:edge], -1, -1)

    tile_place = lax.axis_index("tile")
    col_place = lax.axis_index("col")
    row_weights = blend_ramps(height, (tile_place > 0).astype(f32), (tile_place < tiles - 1).astype(f32))
    col_weights = blend_ramps(columns, (col_place > 0).astype(f32), (col_place < cols - 1).astype(f32))

    group = math.gcd(devices, max(1, 96 // slots))
    whole3 = lambda n: pl.BlockSpec((n, blocks, LANES), lambda i: (0, 0, 0))
    whole2 = lambda n: pl.BlockSpec((n, LANES), lambda i: (0, 0))
    outgoing = pl.pallas_call(
        lambda *refs: blend_and_place(*refs, height=height, per=per),
        grid=(devices // group,),
        in_specs=[
            smem, smem, whole3(3), whole3(height * per), whole2(height * per), whole2(height * per),
            whole3(edge), whole3(edge), whole2(edge), whole2(edge), whole2(edge), whole2(edge),
        ],
        out_specs=pl.BlockSpec((group * slots * per, blocks, LANES), lambda i: (i, 0, 0)),
        out_shape=jax.ShapeDtypeStruct((devices * slots * per, blocks, LANES), f32),
        scratch_shapes=[pltpu.VMEM(((height + 1) * per, blocks, LANES), f32)],
        name="blend_and_place",
    )(
        source, row_weights, col_weights.reshape(3, blocks, LANES), resampled, from_left, from_right,
        from_above, from_below, corner_al, corner_ar, corner_bl, corner_br,
    )
    arrived = lax.all_to_all(outgoing, ("col", "tile"), split_axis=0, concat_axis=0, tiled=True)
    return arrived.reshape(devices * slots, channels, planes, columns)


def solution(mesh):
    placed = (
        P("tile", None, None, "col"),
        P(),
        P("tile", "col", None),
        P("tile", "col", None),
        P("tile", "col", None),
        P("tile", "col", None, None),
    )
    return jax.shard_map(
        shards,
        mesh=mesh,
        in_specs=placed,
        out_specs=P(("col", "tile"), None, None, None),
        check_vma=False,
    )
```

```python
import math

import jax
import jax.numpy as jnp
from jax import lax
from jax.experimental import pallas as pl
from jax.experimental.pallas import tpu as pltpu
from jax.sharding import PartitionSpec as P

MARGIN = 128
LANES = 128
TAPS = (-1, 0, 1, 2)


def cubic_weights(f):
    square = f * f
    cube = square * f
    return (
        -0.5 * cube + square - 0.5 * f,
        1.5 * cube - 2.5 * square + 1.0,
        -1.5 * cube + 2.0 * square + 0.5 * f,
        0.5 * cube - 0.5 * square,
    )


def resample_rows(sub, off, gain, x, field, out, head, tail, left, right, pad, *,
                  height, step_rows, window, pitch, channel):
    step = pl.program_id(0)
    start = jnp.clip(step * step_rows - 4, 0, height - window)
    row_w = cubic_weights(sub[0])
    col_w = cubic_weights(sub[1])
    row_off = off[0]
    col_off = off[1]
    edge_steps = MARGIN // step_rows
    steps = height // step_rows
    blocks = x.shape[2]
    lane = lax.broadcasted_iota(jnp.int32, (blocks, LANES), 1)
    takes_up = [lane < col_off + k for k in TAPS]
    takes_down = [lane >= LANES + col_off + k for k in TAPS]
    turns = [(LANES - col_off - k) & (LANES - 1) for k in TAPS]
    scale = field[0] * gain[channel]

    some = math.gcd(16, step_rows)

    @pl.loop(0, step_rows // some)
    def _(g):
        for u in range(some):
            r = g * some + u
            row = step * step_rows + r
            y = None
            for k, w in zip(TAPS, row_w):
                part = x[jnp.clip(row + row_off + k, 0, height - 1) - start, 0] * w
                y = part if y is None else y + part
            pad[pl.ds(pl.multiple_of(g * (some * pitch), 8) + u * pitch + 8, blocks), :] = y * scale

    last = pad[pl.ds(7 + blocks, step_rows, stride=pitch), :]
    first = pad[pl.ds(8, step_rows, stride=pitch), :]
    pad[pl.ds(8 + blocks, step_rows, stride=pitch), :] = jnp.broadcast_to(last[:, LANES - 1 :], last.shape)
    pad[pl.ds(7, step_rows, stride=pitch), :] = jnp.broadcast_to(first[:, :1], first.shape)

    many = math.gcd(32, step_rows)

    @pl.loop(0, step_rows // many)
    def _(g):
        for u in range(many):
            base = pl.multiple_of(g * (many * pitch), 8) + u * pitch
            y = pad[pl.ds(base + 8, blocks), :]
            up = pad[pl.ds(base + 9, blocks), :]
            down = pad[pl.ds(base + 7, blocks), :]
            z = None
            for k in range(4):
                mixed = jnp.where(takes_up[k], up, jnp.where(takes_down[k], down, y))
                part = pltpu.roll(mixed, turns[k], 1) * col_w[k]
                z = part if z is None else z + part
            out[pl.ds(pl.multiple_of(g * (many * blocks), 8) + u * blocks, blocks), :] = z

    left[...] = out[pl.ds(0, step_rows, stride=blocks), :]
    right[...] = out[pl.ds(blocks - 1, step_rows, stride=blocks), :]

    @pl.when(step < edge_steps)
    def _():
        head[...] = out[...]

    @pl.when(step >= steps - edge_steps)
    def _():
        tail[...] = out[...]


def plan_rows(owner, after, source, count, *, height, slots, devices):
    @pl.loop(0, devices * slots, unroll=8)
    def _(s):
        source[s] = height

    @pl.loop(0, devices)
    def _(d):
        count[d] = 0

    @pl.loop(0, height, unroll=8)
    def _(row):
        d = owner[row]
        rank = count[d]
        count[d] = rank + 1
        source[d * slots + rank] = row


def blend_and_place(source, row_w, col_w, own, left, right, above, below, corner_al, corner_ar,
                    corner_bl, corner_br, out, joined, *, height):
    step = pl.program_id(0)

    @pl.when(step == 0)
    def _():
        before = col_w[0]
        mine = col_w[1]
        after = col_w[2]

        def across(mid, lo, hi, i):
            lo_v = jnp.broadcast_to(lo[pl.ds(i, 1), :], mine.shape)
            hi_v = jnp.broadcast_to(hi[pl.ds(i, 1), :], mine.shape)
            return mine * mid[i] + before * lo_v + after * hi_v

        @pl.loop(0, MARGIN, unroll=16)
        def _(i):
            joined[i] = row_w[1, i] * across(own, left, right, i) + row_w[0, i] * across(
                above, corner_al, corner_ar, i)

        @pl.loop(MARGIN, height - MARGIN, unroll=16)
        def _(i):
            joined[i] = across(own, left, right, i)

        @pl.loop(0, MARGIN, unroll=16)
        def _(t):
            i = t + height - MARGIN
            joined[i] = row_w[1, i] * across(own, left, right, i) + row_w[2, i] * across(
                below, corner_bl, corner_br, t)

        joined[height] = jnp.zeros(joined.shape[1:], jnp.float32)

    here = out.shape[0]

    @pl.loop(0, here, unroll=16)
    def _(s):
        out[s] = joined[source[step * here + s]]


def weave(*refs):
    for p, piece in enumerate(refs[:-1]):
        refs[-1][:, p] = piece[...]


def blend_ramps(length, has_prev, has_next):
    place = jnp.arange(length).astype(jnp.float32)
    rising = jnp.square(jnp.sin(0.5 * math.pi * (place + 0.5) / MARGIN))
    falling = jnp.square(jnp.cos(0.5 * math.pi * (place - (length - MARGIN) + 0.5) / MARGIN))
    head = place < MARGIN
    tail = place >= length - MARGIN
    before = jnp.where(head, has_prev * (1.0 - rising), 0.0)
    own = jnp.where(
        head,
        has_prev * rising + 1.0 - has_prev,
        jnp.where(tail, has_next * falling + 1.0 - has_next, 1.0),
    )
    after = jnp.where(tail, has_next * (1.0 - falling), 0.0)
    return jnp.stack([before, own, after])


def shards(acquired, flatfield, tile_gain, subvoxel, band_offset, row_owner):
    height, channels, planes, columns = acquired.shape
    per = channels * planes
    blocks = columns // LANES
    cols, tiles = lax.axis_size("col"), lax.axis_size("tile")
    devices = cols * tiles
    slots = max(2, (3 * height + 2 * devices - 1) // (2 * devices))
    f32 = jnp.float32
    smem = pl.BlockSpec(memory_space=pltpu.SMEM)
    step_rows = math.gcd(MARGIN, height)
    steps = height // step_rows
    window = step_rows + 8
    pitch = blocks + 8
    sub = subvoxel.reshape(2)
    off = band_offset.reshape(2)
    gain = tile_gain.reshape(channels)
    voxels = acquired.reshape(height, per, blocks, LANES)
    field = flatfield.reshape(channels, blocks, LANES)

    def resample(p):
        channel = p // planes
        return pl.pallas_call(
            lambda *refs: resample_rows(*refs, height=height, step_rows=step_rows, window=window,
                                        pitch=pitch, channel=channel),
            grid=(steps,),
            in_specs=[
                smem, smem, smem,
                pl.BlockSpec(
                    (pl.Element(window), pl.Element(1), pl.Element(blocks), pl.Element(LANES)),
                    lambda i: (jnp.clip(i * step_rows - 4, 0, height - window), p, 0, 0)),
                pl.BlockSpec((1, blocks, LANES), lambda i: (channel, 0, 0)),
            ],
            out_specs=[
                pl.BlockSpec((step_rows * blocks, LANES), lambda i: (i, 0)),
                pl.BlockSpec((step_rows * blocks, LANES), lambda i: (jnp.minimum(i, MARGIN // step_rows - 1), 0)),
                pl.BlockSpec((step_rows * blocks, LANES),
                             lambda i: (jnp.maximum(i - (steps - MARGIN // step_rows), 0), 0)),
                pl.BlockSpec((step_rows, LANES), lambda i: (i, 0)),
                pl.BlockSpec((step_rows, LANES), lambda i: (i, 0)),
            ],
            out_shape=[
                jax.ShapeDtypeStruct((height * blocks, LANES), f32),
                jax.ShapeDtypeStruct((MARGIN * blocks, LANES), f32),
                jax.ShapeDtypeStruct((MARGIN * blocks, LANES), f32),
                jax.ShapeDtypeStruct((height, LANES), f32),
                jax.ShapeDtypeStruct((height, LANES), f32),
            ],
            scratch_shapes=[pltpu.VMEM((step_rows * pitch + 16, LANES), f32)],
            name=f"resample_rows_{p}",
        )(sub, off, gain, voxels, field)

    def shifted(value, dc, dt):
        pairs = []
        for c in range(cols):
            for t in range(tiles):
                if 0 <= c + dc < cols and 0 <= t + dt < tiles:
                    pairs.append((c * tiles + t, (c + dc) * tiles + t + dt))
        return lax.ppermute(value, ("col", "tile"), pairs)

    def halo(pieces):
        _, head, tail, left, right = pieces
        return (
            shifted(right, 1, 0),
            shifted(left, -1, 0),
            shifted(tail, 0, 1).reshape(MARGIN, blocks, LANES),
            shifted(head, 0, -1).reshape(MARGIN, blocks, LANES),
            shifted(right[-MARGIN:], 1, 1),
            shifted(left[-MARGIN:], -1, 1),
            shifted(right[:MARGIN], 1, -1),
            shifted(left[:MARGIN], -1, -1),
        )

    made = [resample(p) for p in range(per)]
    halos = [halo(pieces) for pieces in made]
    source = pl.pallas_call(
        lambda *refs: plan_rows(*refs, height=height, slots=slots, devices=devices),
        in_specs=[smem, pl.BlockSpec(memory_space=pl.ANY)],
        out_specs=smem,
        out_shape=jax.ShapeDtypeStruct((devices * slots,), jnp.int32),
        scratch_shapes=[pltpu.SMEM((devices,), jnp.int32)],
        name="plan_rows",
    )(row_owner.reshape(height), made[0][3])

    tile_place = lax.axis_index("tile")
    col_place = lax.axis_index("col")
    row_weights = blend_ramps(height, (tile_place > 0).astype(f32), (tile_place < tiles - 1).astype(f32))
    col_weights = blend_ramps(columns, (col_place > 0).astype(f32), (col_place < cols - 1).astype(f32))
    col_weights = col_weights.reshape(3, blocks, LANES)

    group = math.gcd(devices, max(1, 192 // slots))
    whole3 = lambda n: pl.BlockSpec((n, blocks, LANES), lambda i: (0, 0, 0))
    whole2 = lambda n: pl.BlockSpec((n, LANES), lambda i: (0, 0))

    def place(p):
        return pl.pallas_call(
            lambda *refs: blend_and_place(*refs, height=height),
            grid=(devices // group,),
            in_specs=[
                smem, smem, whole3(3), whole3(height), whole2(height), whole2(height),
                whole3(MARGIN), whole3(MARGIN), whole2(MARGIN), whole2(MARGIN), whole2(MARGIN), whole2(MARGIN),
            ],
            out_specs=pl.BlockSpec((group * slots, blocks, LANES), lambda i: (i, 0, 0)),
            out_shape=jax.ShapeDtypeStruct((devices * slots, blocks, LANES), f32),
            scratch_shapes=[pltpu.VMEM((height + 1, blocks, LANES), f32)],
            name=f"blend_and_place_{p}",
        )(source, row_weights, col_weights, made[p][0].reshape(height, blocks, LANES), *halos[p])

    arrived = [
        lax.all_to_all(place(p), ("col", "tile"), split_axis=0, concat_axis=0, tiled=True) for p in range(per)
    ]
    chunk = math.gcd(devices * slots, 96)
    woven = pl.pallas_call(
        weave,
        grid=(devices * slots // chunk,),
        in_specs=[pl.BlockSpec((chunk, blocks, LANES), lambda i: (i, 0, 0))] * per,
        out_specs=pl.BlockSpec((chunk, per, blocks, LANES), lambda i: (i, 0, 0, 0)),
        out_shape=jax.ShapeDtypeStruct((devices * slots, per, blocks, LANES), f32),
        name="weave",
    )(*arrived)
    return woven.reshape(devices * slots, channels, planes, columns)


def solution(mesh):
    placed = (
        P("tile", None, None, "col"),
        P(),
        P("tile", "col", None),
        P("tile", "col", None),
        P("tile", "col", None),
        P("tile", "col", None, None),
    )
    return jax.shard_map(
        shards,
        mesh=mesh,
        in_specs=placed,
        out_specs=P(("col", "tile"), None, None, None),
        check_vma=False,
    )
```
